32 devices in a mesh: sensor: 4 (over y, core), space: 8 (over z, x).
Axes of the slice: x: 2, y: 2, z: 4, core: 2. Of those that a mesh axis runs over, the one named last changes fastest.
Arguments:
- jacobian: float32 [512, 16384], P('space', 'sensor'), as said below
- residual: float32 [16384], P('sensor'), may hold values from -6 to 6
- damping: float32 [1], replicated, may hold values from 0.3 to 3
Outputs:
- update: float32 [512], replicated
The draws below stay inside these ranges and needn't reach their ends.
Inputs may be any that keep to these rules, and one draw needn't show every extreme that they name: `jacobian`: every column block of the Jacobian has full rank over any 512 observations, which number at least the parameters; the entries are real-valued with row and column scales that vary.
All inputs are finite; a program needn't handle non-finite values.
Results may differ from the reference program's by a relative error of at most 0.00011.
Values sent between devices are 32-bit elements; how exact they have to be, the bound alone decides.
No kernel may reach another device: no remote copies, remote signals or barrier semaphores. Data moves between devices by JAX's collectives and lax.ppermute only.
A program may use at most 64 MiB of HBM per device.

```python
import math
import jax
import jax.numpy as jnp
from jax import lax

P_SIZE = 512
M = 16384


def draw_jacobian(key, part):
    first_key, second_key, third_key = jax.random.split(jax.random.fold_in(key, 17), 3)
    row_scale = jnp.exp(jax.random.uniform(first_key, (1, M), jnp.float32) * jnp.log(10.0))
    col_scale = 0.1 * jnp.exp(jax.random.uniform(second_key, (P_SIZE, 1), jnp.float32) * jnp.log(10.0))
    base = jax.random.normal(third_key, (P_SIZE, M), jnp.float32)
    return (base * row_scale * col_scale / (4.0 * jnp.sqrt(float(M)))).astype(jnp.float32)


def level_of(own_key, dims, cuts, least, high):
    gain, own = 1.0, jax.random.fold_in(own_key, 6)
    for dim, parts in cuts:
        heights = jnp.exp(jax.random.uniform(jax.random.fold_in(own, dim), (parts,), jnp.float32, least / len(cuts), high / len(cuts)))
        gain = gain * jnp.repeat(heights, dims[dim] // parts).reshape([-1 if axis == dim else 1 for axis in range(len(dims))])
    return gain


def gaussian(stream_key, shape, width, bound, pieces=(), kind=jnp.bfloat16):
    values = width * jax.random.normal(stream_key, shape, jnp.float32)
    if pieces:
        values = values * level_of(stream_key, shape, pieces, -0.22, 0.18)
    return jnp.clip(values, -bound, bound).astype(kind)


def setup_inputs(seed: int = 0) -> dict:
    streams_of = jax.random.split(jax.random.key(seed), 4)
    return {
        "jacobian": draw_jacobian(jax.random.fold_in(streams_of[3], 71), 0),
        "residual": gaussian(streams_of[1], (M,), 1.0, 6.0, ((0, 4),), jnp.float32),
        "damping": jnp.clip(jnp.exp(jax.random.uniform(streams_of[2], (1,), jnp.float32, math.log(0.3), math.log(3.0))), 0.3, 3.0),
    }


def reference(jacobian, residual, damping):
    gram = lax.dot_general(jacobian.astype(jnp.float32), jacobian.astype(jnp.float32), (((1,), (1,)), ((), ())), precision=lax.Precision.HIGHEST, preferred_element_type=jnp.float32)
    grad = jnp.dot(jacobian.astype(jnp.float32), residual.astype(jnp.float32), precision=lax.Precision.HIGHEST, preferred_element_type=jnp.float32)
    damped = gram + damping[0] * jnp.diag(jnp.diag(gram))
    factor = jnp.linalg.cholesky(damped)
    return -jax.scipy.linalg.cho_solve((factor, True), grad)
```

```python
import functools

import jax
import jax.numpy as jnp
from jax import lax
from jax.experimental import pallas as pl
from jax.experimental.pallas import tpu as pltpu
from jax.sharding import PartitionSpec as P

B = 128
VMEM = pl.BlockSpec(memory_space=pltpu.VMEM)
SMEM = pl.BlockSpec(memory_space=pltpu.SMEM)


def f32(*shape):
    return jax.ShapeDtypeStruct(shape, jnp.float32)


def dot(a, b, dims=((1,), (0,))):
    return lax.dot_general(
        a, b, (dims, ((), ())), precision=lax.Precision.HIGHEST, preferred_element_type=jnp.float32
    )


def panel_starts(size):
    starts = [0]
    for k in range(size // B):
        starts.append(starts[-1] + size - k * B)
    return starts


def gram_kernel(order, total, *refs):
    residual_ref, own_ref, *got = refs[: len(order) + 2]
    keep_ref, send_ref, rows_ref, pack_ref = refs[len(order) + 2 :]
    me, core = lax.axis_index("space"), lax.rem(lax.axis_index("sensor"), 2)
    size = rows_ref.shape[0]
    part = own_ref.shape[0]
    for step, ref in zip([0] + order, [own_ref] + got):
        at = pl.multiple_of(jnp.bitwise_xor(me, step) * part, part)
        rows_ref[pl.ds(at, part), :] = ref[...]
    starts = panel_starts(size)
    for k in range(size // B):
        pack_ref[starts[k] : starts[k + 1], :] = dot(
            rows_ref[k * B :, :], rows_ref[k * B : (k + 1) * B, :], ((1,), (1,))
        )
    grad = dot(jnp.broadcast_to(residual_ref[...], (8, residual_ref.shape[1])), rows_ref[...], ((1,), (1,)))
    tail = starts[-1]
    pack_ref[tail:total, :] = jnp.zeros((total - tail, B), jnp.float32)
    for k in range(size // B):
        pack_ref[tail + k : tail + k + 1, :] = grad[0:1, k * B : (k + 1) * B]
    half = total // 2
    keep_ref[...] = pack_ref[pl.ds(pl.multiple_of(core * half, 8), half), :]
    send_ref[...] = pack_ref[pl.ds(pl.multiple_of((1 - core) * half, 8), half), :]


def plane_index():
    return lax.div(lax.axis_index("sensor"), 2) * 2 + lax.rem(lax.axis_index("space"), 2)


def split_kernel(keep_ref, got_ref, *refs):
    *outs, sum_ref = refs
    sum_ref[...] = keep_ref[...] + got_ref[...]
    me, part = plane_index(), outs[0].shape[0]
    for t, out in enumerate(outs):
        out[...] = sum_ref[pl.ds(pl.multiple_of(jnp.bitwise_xor(me, t) * part, part), part), :]


def join_kernel(*refs):
    *parts, out_ref = refs
    me, part = plane_index(), parts[0].shape[0]
    for t, ref in enumerate(parts):
        out_ref[pl.ds(pl.multiple_of(jnp.bitwise_xor(me, t) * part, part), part), :] = ref[...]


def lanes(x, l):
    return jnp.broadcast_to(x[:, l : l + 1], x.shape)


def subs(x, s):
    return jnp.broadcast_to(x[s : s + 1, :], x.shape)


def inverse(tiles, zero, width=16):
    tiles = list(tiles)
    n, h = len(tiles), width // 8
    lane = lax.broadcasted_iota(jnp.int32, tiles[0].shape, 1)
    sub = lax.broadcasted_iota(jnp.int32, tiles[0].shape, 0)
    for m in range(0, n, h):
        base = 8 * m
        rows = tiles[m : m + h]
        wide = [[lanes(rows[q], base + c) + zero for q in range(h)] for c in range(width)]
        for c in range(width):
            q0, s = divmod(c, 8)
            inv = 1.0 / subs(wide[c][q0], s)
            head = sub == s
            at = lane == base + c
            unit = jnp.where(head, 1.0, 0.0)
            rows = [jnp.where(at, unit if q == q0 else 0.0, rows[q]) for q in range(h)]
            for block in wide[c + 1 :] + [rows]:
                t = subs(block[q0], s) * inv
                for q in range(h):
                    rest = block[q] - wide[c][q] * t
                    block[q] = jnp.where(head, t, rest) if q == q0 else rest
        w = [subs(rows[c // 8], c % 8) for c in range(width)]
        keep = (lane < base) | (lane >= base + width)
        for i in list(range(m + h, n)) + list(range(m)):
            t = [lanes(tiles[i], base + c) * w[c] for c in range(width)]
            while len(t) > 1:
                t = [a + b for a, b in zip(t[::2], t[1::2])]
            tiles[i] = jnp.where(keep, tiles[i], 0.0) - t[0]
        tiles[m : m + h] = rows
    return tiles


def solve_kernel(size, damp_ref, mine_ref, other_ref, x_ref, pack_ref, d_ref, v_ref, *panels):
    nb = size // B
    w_refs, z_refs = panels[:nb], panels[nb:]
    core = lax.rem(lax.axis_index("sensor"), 2)
    half = mine_ref.shape[0]
    pack_ref[pl.ds(pl.multiple_of(core * half, 8), half), :] = mine_ref[...]
    pack_ref[pl.ds(pl.multiple_of((1 - core) * half, 8), half), :] = other_ref[...]
    starts = panel_starts(size)
    factor = damp_ref[0]
    zero = jnp.minimum(jnp.full((8, B), jnp.abs(factor)), 0.0)
    lane = lax.broadcasted_iota(jnp.int32, (8, B), 1)
    sub = lax.broadcasted_iota(jnp.int32, (8, B), 0)
    for k, w_ref in enumerate(w_refs):
        rows = size - k * B
        w_ref[0:rows, :] = pack_ref[starts[k] : starts[k + 1], :]
        w_ref[rows : rows + 8, :] = jnp.broadcast_to(pack_ref[starts[-1] + k : starts[-1] + k + 1, :], (8, B))
        for t in range(B // 8):
            a = w_ref[8 * t : 8 * t + 8, :]
            w_ref[8 * t : 8 * t + 8, :] = a + jnp.where(lane == sub + 8 * t, a * factor, 0.0)
    d_ref[...] = w_refs[0][0:B, :]

    def step(i, carry):
        inv = inverse([d_ref[8 * t : 8 * t + 8, :] for t in range(B // 8)], zero)
        for t in range(B // 8):
            v_ref[8 * t : 8 * t + 8, :] = inv[t]
        for k in range(nb):

            @pl.when(i == k)
            def _():
                z_refs[k][...] = dot(w_refs[k][B:, :], v_ref[...])
                for j in range(k + 1, nb):
                    at = (j - k) * B
                    new = w_refs[j][...] - dot(
                        z_refs[k][at - B :, :], w_refs[k][at : at + B, :], ((1,), (1,))
                    )
                    if j == k + 1:
                        d_ref[...] = new[0:B]
                    w_refs[j][...] = new

        return carry

    lax.fori_loop(0, nb, step, 0)
    x = [None] * nb
    for k in reversed(range(nb)):
        below = (nb - 1 - k) * B
        s = z_refs[k][below : below + 8, :]
        for j in range(k + 1, nb):
            s = s - dot(x[j], z_refs[k][(j - k - 1) * B : (j - k) * B, :])
        x[k] = s
        x_ref[0:1, k * B : (k + 1) * B] = -s[0:1]


def tree_sum(parts):
    while len(parts) > 1:
        parts = [a + b for a, b in zip(parts[::2], parts[1::2])]
    return parts[0]


def per_device(jacobian, residual, damping):
    sensors, spaces = lax.axis_size("sensor"), lax.axis_size("space")
    part, seen = jacobian.shape
    size = part * spaces
    span = seen // spaces
    me = lax.axis_index("space")
    both = ("sensor", "space")

    def swap(x, bits):
        return lax.ppermute(x, both, [(i, i ^ bits) for i in range(sensors * spaces)])

    def panel(step):
        return lax.dynamic_slice_in_dim(jacobian, (me ^ step) * span, span, 1)

    order = list(range(spaces // 2, spaces)) + list(range(1, spaces // 2))
    got = [swap(panel(step), step) for step in order]
    seen_residual = lax.dynamic_slice_in_dim(residual, me * span, span, 0).reshape(1, span)

    blocks = panel_starts(size)[-1]
    unit = 16 * sensors
    total = -(-(blocks + size // B) // unit) * unit
    half = total // 2
    quarter = half // sensors
    keep, send = pl.pallas_call(
        functools.partial(gram_kernel, order, total),
        out_shape=(f32(half, B), f32(half, B)),
        in_specs=[VMEM] * (spaces + 1),
        out_specs=(VMEM, VMEM),
        scratch_shapes=[pltpu.VMEM((size, span), jnp.float32), pltpu.VMEM((total, B), jnp.float32)],
        name="gram",
    )(seen_residual, panel(0), *got)
    pieces = pl.pallas_call(
        split_kernel,
        out_shape=[f32(quarter, B)] * sensors,
        in_specs=[VMEM] * 2,
        out_specs=[VMEM] * sensors,
        scratch_shapes=[pltpu.VMEM((half, B), jnp.float32)],
        name="split",
    )(keep, swap(send, spaces))
    plane = [(t >> 1) * 2 * spaces + (t & 1) for t in range(sensors)]
    mine = tree_sum([pieces[0]] + [swap(pieces[t], plane[t]) for t in range(1, sensors)])
    mine = tree_sum([mine] + [swap(mine, 2 * u) for u in range(1, spaces // 2)])
    mine = pl.pallas_call(
        join_kernel,
        out_shape=f32(half, B),
        in_specs=[VMEM] * sensors,
        out_specs=VMEM,
        name="join",
    )(mine, *[swap(mine, plane[t]) for t in range(1, sensors)])
    nb = size // B
    scratch = lambda rows: pltpu.VMEM((rows, B), jnp.float32)
    x = pl.pallas_call(
        functools.partial(solve_kernel, size),
        out_shape=f32(1, size),
        in_specs=[SMEM, VMEM, VMEM],
        out_specs=VMEM,
        scratch_shapes=[scratch(total), scratch(B), scratch(B)]
        + [scratch(size - k * B + 8) for k in range(nb)]
        + [scratch(size - (k + 1) * B + 8) for k in range(nb)],
        name="solve",
    )(damping, mine, swap(mine, spaces))
    return x.reshape(size)


def solution(mesh):
    placed = (P("space", "sensor"), P("sensor"), P())
    return jax.shard_map(per_device, mesh=mesh, in_specs=placed, out_specs=P(), check_vma=False)
```

```python
import functools

import jax
import jax.numpy as jnp
from jax import lax
from jax.experimental import pallas as pl
from jax.experimental.pallas import tpu as pltpu
from jax.sharding import PartitionSpec as P

B = 128
VMEM = pl.BlockSpec(memory_space=pltpu.VMEM)
SMEM = pl.BlockSpec(memory_space=pltpu.SMEM)
ANY = pl.BlockSpec(memory_space=pl.ANY)
KERNEL_VMEM = 16 << 20


def f32(*shape):
    return jax.ShapeDtypeStruct(shape, jnp.float32)


def dot(a, b, dims=((1,), (0,))):
    return lax.dot_general(
        a, b, (dims, ((), ())), precision=lax.Precision.HIGHEST, preferred_element_type=jnp.float32
    )


def panel_starts(size):
    starts = [0]
    for k in range(size // B):
        starts.append(starts[-1] + size - k * B)
    return starts


def plane_index():
    return lax.div(lax.axis_index("sensor"), 2) * 2 + lax.rem(lax.axis_index("space"), 2)


def piece_rows(t, own, half, piece):
    core = lax.rem(lax.axis_index("sensor"), 2)
    side = core if own else 1 - core
    return pl.ds(pl.multiple_of(side * half + jnp.bitwise_xor(plane_index(), t) * piece, 8), piece)


def run_copies(pairs, sems):
    copies = [pltpu.make_async_copy(src, dst, sems.at[i]) for i, (src, dst) in enumerate(pairs)]
    for copy in copies:
        copy.start()
    return copies


def gram_kernel(order, total, pieces, *refs):
    n = len(order)
    residual_ref, own_ref, *got = refs[: n + 2]
    outs = refs[n + 2 : n + 2 + 2 * pieces]
    rows_ref, pack_ref, in_sems, out_sems = refs[n + 2 + 2 * pieces :]
    me = lax.axis_index("space")
    size, span = rows_ref.shape
    part = own_ref.shape[0]
    own = own_ref.at[:, pl.ds(pl.multiple_of(me * span, span), span)]
    at = [pl.ds(pl.multiple_of(jnp.bitwise_xor(me, step) * part, part), part) for step in [0] + order]
    for copy in run_copies([(src, rows_ref.at[rows]) for src, rows in zip([own] + got, at)], in_sems):
        copy.wait()
    starts = panel_starts(size)
    wide = 2 * B if size % (2 * B) == 0 else B
    for lo in range(0, size, wide):
        gram = dot(rows_ref[lo:, :], rows_ref[lo : lo + wide, :], ((1,), (1,)))
        for skip in range(0, wide, B):
            k = (lo + skip) // B
            pack_ref[starts[k] : starts[k + 1], :] = gram[skip:, skip : skip + B]
    grad = dot(jnp.broadcast_to(residual_ref[...], (8, span)), rows_ref[...], ((1,), (1,)))
    tail = starts[-1]
    pack_ref[tail:total, :] = jnp.zeros((total - tail, B), jnp.float32)
    for k in range(size // B):
        pack_ref[tail + k : tail + k + 1, :] = grad[0:1, k * B : (k + 1) * B]
    half = total // 2
    piece = half // pieces
    spots = [piece_rows(t, own, half, piece) for own in (False, True) for t in range(pieces)]
    for copy in run_copies([(pack_ref.at[rows], out) for rows, out in zip(spots, outs)], out_sems):
        copy.wait()


def lanes(x, l):
    return jnp.broadcast_to(x[:, l : l + 1], x.shape)


def subs(x, s):
    return jnp.broadcast_to(x[s : s + 1, :], x.shape)


def inverse(tiles, zero, width=16):
    tiles = list(tiles)
    n, h = len(tiles), width // 8
    lane = lax.broadcasted_iota(jnp.int32, tiles[0].shape, 1)
    sub = lax.broadcasted_iota(jnp.int32, tiles[0].shape, 0)
    blank = jnp.zeros_like(tiles[0])
    for m in range(0, n, h):
        base = 8 * m
        rows = tiles[m : m + h]
        wide = [[lanes(rows[q], base + c) + zero for q in range(h)] for c in range(width)]
        unscaled = [[blank] * h, [blank] * h]
        for c in range(0, width, 2):
            q0, s = divmod(c, 8)
            first, second = sub == s, sub == s + 1
            pair = first | second
            one, two = wide[c], wide[c + 1]
            p11, p21, p22 = subs(one[q0], s), subs(one[q0], s + 1), subs(two[q0], s + 1)
            inv = 1.0 / (p11 * p22 - p21 * p21)
            left = [(one[q] * p22 - two[q] * p21) * inv for q in range(h)]
            right = [(two[q] * p11 - one[q] * p21) * inv for q in range(h)]
            left[q0], right[q0] = jnp.where(pair, 0.0, left[q0]), jnp.where(pair, 0.0, right[q0])
            unscaled[0][q0] = jnp.where(pair, jnp.where(first, p22, p11) * inv, unscaled[0][q0])
            unscaled[1][q0] = jnp.where(pair, p21 * inv, unscaled[1][q0])
            at, at2 = lane == base + c, lane == base + c + 1
            rows = [jnp.where(at | at2, 0.0, rows[q]) for q in range(h)]
            rows[q0] = jnp.where((at & first) | (at2 & second), 1.0, rows[q0])
            for block in wide[c + 2 :] + [rows]:
                a, b = subs(block[q0], s), subs(block[q0], s + 1)
                for q in range(h):
                    block[q] = block[q] - (left[q] * a + right[q] * b)
        even = (sub & 1) == 0
        swapped = [jnp.where(even, pltpu.roll(rows[q], 7, 0), pltpu.roll(rows[q], 1, 0)) for q in range(h)]
        rows = [rows[q] * unscaled[0][q] - swapped[q] * unscaled[1][q] for q in range(h)]
        w = [subs(rows[c // 8], c % 8) for c in range(width)]
        keep = (lane < base) | (lane >= base + width)
        near = list(range(m + h, min(m + 2 * h, n)))
        far = [i for i in list(range(m + 2 * h, n)) + list(range(m))]
        for i in near:
            t = [lanes(tiles[i], base + c) * w[c] for c in range(width)]
            while len(t) > 1:
                t = [a + b for a, b in zip(t[::2], t[1::2])]
            tiles[i] = jnp.where(keep, tiles[i], 0.0) - t[0]
        padded = jnp.concatenate([rows[i - m] if m <= i < m + h else blank for i in range(n)], 0)
        change = dot(jnp.concatenate([tiles[i] for i in far], 0), padded)
        for j, i in enumerate(far):
            tiles[i] = jnp.where(keep, tiles[i], 0.0) - change[8 * j : 8 * j + 8]
        tiles[m : m + h] = rows
    return tiles


def solve_kernel(size, pieces, damp_ref, *refs):
    nb = size // B
    got, x_ref, (pack_ref, sems, d_ref, v_ref, *panels) = refs[: 2 * pieces], refs[2 * pieces], refs[2 * pieces + 1 :]
    w_refs, z_refs = panels[:nb], panels[nb:]
    piece = got[0].shape[0]
    spots = [piece_rows(t, own, piece * pieces, piece) for own in (True, False) for t in range(pieces)]
    for copy in run_copies([(ref, pack_ref.at[rows]) for ref, rows in zip(got, spots)], sems):
        copy.wait()
    starts = panel_starts(size)
    factor = damp_ref[0]
    zero = jnp.minimum(jnp.full((8, B), jnp.abs(factor)), 0.0)
    lane = lax.broadcasted_iota(jnp.int32, (8, B), 1)
    sub = lax.broadcasted_iota(jnp.int32, (8, B), 0)
    for k, w_ref in enumerate(w_refs):
        rows = size - k * B
        w_ref[0:rows, :] = pack_ref[starts[k] : starts[k + 1], :]
        w_ref[rows : rows + 8, :] = jnp.broadcast_to(pack_ref[starts[-1] + k : starts[-1] + k + 1, :], (8, B))
        for t in range(B // 8):
            a = w_ref[8 * t : 8 * t + 8, :]
            w_ref[8 * t : 8 * t + 8, :] = a + jnp.where(lane == sub + 8 * t, a * factor, 0.0)
    d_ref[...] = w_refs[0][0:B, :]

    def step(i, carry):
        inv = inverse([d_ref[8 * t : 8 * t + 8, :] for t in range(B // 8)], zero)
        for t in range(B // 8):
            v_ref[8 * t : 8 * t + 8, :] = inv[t]
        for k in range(nb):

            @pl.when(i == k)
            def _():
                z_refs[k][...] = dot(w_refs[k][B:, :], v_ref[...])
                for j in range(k + 1, nb):
                    at = (j - k) * B
                    new = w_refs[j][...] - dot(
                        z_refs[k][at - B :, :], w_refs[k][at : at + B, :], ((1,), (1,))
                    )
                    if j == k + 1:
                        d_ref[...] = new[0:B]
                    w_refs[j][...] = new

        return carry

    lax.fori_loop(0, nb, step, 0)
    x = [None] * nb
    for k in reversed(range(nb)):
        below = (nb - 1 - k) * B
        s = z_refs[k][below : below + 8, :]
        for j in range(k + 1, nb):
            s = s - dot(x[j], z_refs[k][(j - k - 1) * B : (j - k) * B, :])
        x[k] = s
        x_ref[0:1, k * B : (k + 1) * B] = -s[0:1]


def solve_call(size, total, damping, got):
    nb = size // B
    scratch = lambda rows: pltpu.VMEM((rows, B), jnp.float32)
    return pl.pallas_call(
        functools.partial(solve_kernel, size, len(got) // 2),
        out_shape=f32(1, size),
        in_specs=[SMEM] + [ANY] * len(got),
        out_specs=VMEM,
        scratch_shapes=[scratch(total), pltpu.SemaphoreType.DMA((len(got),)), scratch(B), scratch(B)]
        + [scratch(size - k * B + 8) for k in range(nb)]
        + [scratch(size - (k + 1) * B + 8) for k in range(nb)],
        compiler_params=pltpu.CompilerParams(vmem_limit_bytes=KERNEL_VMEM),
        name="solve",
    )(damping, *got)


def tree_sum(parts):
    while len(parts) > 1:
        parts = [a + b for a, b in zip(parts[::2], parts[1::2])]
    return parts[0]


def per_device(jacobian, residual, damping):
    sensors, spaces = lax.axis_size("sensor"), lax.axis_size("space")
    part, seen = jacobian.shape
    size = part * spaces
    span = seen // spaces
    me = lax.axis_index("space")
    both = ("sensor", "space")

    def swap(x, bits):
        return lax.ppermute(x, both, [(i, i ^ bits) for i in range(sensors * spaces)])

    def panel(step):
        return lax.dynamic_slice_in_dim(jacobian, (me ^ step) * span, span, 1)

    order = list(range(spaces // 2, spaces)) + list(range(1, spaces // 2))
    got = [swap(panel(step), step) for step in order]
    seen_residual = lax.dynamic_slice_in_dim(residual, me * span, span, 0).reshape(1, span)

    blocks = panel_starts(size)[-1]
    unit = 16 * sensors
    total = -(-(blocks + size // B) // unit) * unit
    pieces = sensors
    piece = total // 2 // pieces
    packed = pl.pallas_call(
        functools.partial(gram_kernel, order, total, pieces),
        out_shape=[f32(piece, B)] * (2 * pieces),
        in_specs=[VMEM] + [ANY] * spaces,
        out_specs=[ANY] * (2 * pieces),
        scratch_shapes=[
            pltpu.VMEM((size, span), jnp.float32),
            pltpu.VMEM((total, B), jnp.float32),
            pltpu.SemaphoreType.DMA((spaces,)),
            pltpu.SemaphoreType.DMA((2 * pieces,)),
        ],
        compiler_params=pltpu.CompilerParams(vmem_limit_bytes=KERNEL_VMEM),
        name="gram",
    )(seen_residual, jacobian, *got)
    plane = [(t >> 1) * 2 * spaces + (t & 1) for t in range(pieces)]
    sums = [kept + swap(sent, spaces) for sent, kept in zip(packed[:pieces], packed[pieces:])]
    mine = tree_sum([sums[0]] + [swap(sums[t], plane[t]) for t in range(1, pieces)])
    mine = tree_sum([mine] + [swap(mine, 2 * u) for u in range(1, spaces // 2)])
    half = [mine] + [swap(mine, plane[t]) for t in range(1, pieces)]
    x = solve_call(size, total, damping, half + [swap(x, spaces) for x in half])
    return x.reshape(size)


def solution(mesh):
    placed = (P("space", "sensor"), P("sensor"), P())
    return jax.shard_map(per_device, mesh=mesh, in_specs=placed, out_specs=P(), check_vma=False)
```

```python
import functools

import jax
import jax.numpy as jnp
from jax import lax
from jax.experimental import pallas as pl
from jax.experimental.pallas import tpu as pltpu
from jax.sharding import PartitionSpec as P

B = 128
VMEM = pl.BlockSpec(memory_space=pltpu.VMEM)
SMEM = pl.BlockSpec(memory_space=pltpu.SMEM)
ANY = pl.BlockSpec(memory_space=pl.ANY)
KERNEL_VMEM = 16 << 20


def f32(*shape):
    return jax.ShapeDtypeStruct(shape, jnp.float32)


def dot(a, b, dims=((1,), (0,))):
    return lax.dot_general(
        a, b, (dims, ((), ())), precision=lax.Precision.HIGHEST, preferred_element_type=jnp.float32
    )


def panel_starts(size):
    starts = [0]
    for k in range(size // B):
        starts.append(starts[-1] + size - k * B)
    return starts


def plane_index():
    return lax.div(lax.axis_index("sensor"), 2) * 2 + lax.rem(lax.axis_index("space"), 2)


def piece_rows(t, own, half, piece):
    core = lax.rem(lax.axis_index("sensor"), 2)
    side = core if own else 1 - core
    return pl.ds(pl.multiple_of(side * half + jnp.bitwise_xor(plane_index(), t) * piece, 8), piece)


def gram_kernel(order, total, pieces, *refs):
    n = len(order)
    residual_ref, own_ref, *got = refs[: n + 2]
    outs = refs[n + 2 : n + 2 + 2 * pieces]
    rows_ref, pack_ref = refs[n + 2 + 2 * pieces :]
    me = lax.axis_index("space")
    size, span = rows_ref.shape
    part = own_ref.shape[0]
    for step, ref in zip([0] + order, [own_ref] + got):
        rows_ref[pl.ds(pl.multiple_of(jnp.bitwise_xor(me, step) * part, part), part), :] = ref[...]
    starts = panel_starts(size)
    wide = 2 * B if size % (2 * B) == 0 else B
    for lo in range(0, size, wide):
        gram = dot(rows_ref[lo:, :], rows_ref[lo : lo + wide, :], ((1,), (1,)))
        for skip in range(0, wide, B):
            k = (lo + skip) // B
            pack_ref[starts[k] : starts[k + 1], :] = gram[skip:, skip : skip + B]
    grad = dot(jnp.broadcast_to(residual_ref[...], (8, span)), rows_ref[...], ((1,), (1,)))
    tail = starts[-1]
    pack_ref[tail:total, :] = jnp.zeros((total - tail, B), jnp.float32)
    for k in range(size // B):
        pack_ref[tail + k : tail + k + 1, :] = grad[0:1, k * B : (k + 1) * B]
    half = total // 2
    piece = half // pieces
    spots = [piece_rows(t, own, half, piece) for own in (False, True) for t in range(pieces)]
    for rows, out in zip(spots, outs):
        out[...] = pack_ref[rows, :]


def lanes(x, l):
    return jnp.broadcast_to(x[:, l : l + 1], x.shape)


def subs(x, s):
    return jnp.broadcast_to(x[s : s + 1, :], x.shape)


def inverse(tiles, zero, width=16):
    tiles = list(tiles)
    n, h = len(tiles), width // 8
    lane = lax.broadcasted_iota(jnp.int32, tiles[0].shape, 1)
    sub = lax.broadcasted_iota(jnp.int32, tiles[0].shape, 0)
    blank = jnp.zeros_like(tiles[0])
    for m in range(0, n, h):
        base = 8 * m
        rows = tiles[m : m + h]
        wide = [[lanes(rows[q], base + c) + zero for q in range(h)] for c in range(width)]
        unscaled = [[blank] * h, [blank] * h]
        for c in range(0, width, 2):
            q0, s = divmod(c, 8)
            first, second = sub == s, sub == s + 1
            pair = first | second
            one, two = wide[c], wide[c + 1]
            p11, p21, p22 = subs(one[q0], s), subs(one[q0], s + 1), subs(two[q0], s + 1)
            inv = 1.0 / (p11 * p22 - p21 * p21)
            left = [(one[q] * p22 - two[q] * p21) * inv for q in range(h)]
            right = [(two[q] * p11 - one[q] * p21) * inv for q in range(h)]
            left[q0], right[q0] = jnp.where(pair, 0.0, left[q0]), jnp.where(pair, 0.0, right[q0])
            unscaled[0][q0] = jnp.where(pair, jnp.where(first, p22, p11) * inv, unscaled[0][q0])
            unscaled[1][q0] = jnp.where(pair, p21 * inv, unscaled[1][q0])
            at, at2 = lane == base + c, lane == base + c + 1
            rows = [jnp.where(at | at2, 0.0, rows[q]) for q in range(h)]
            rows[q0] = jnp.where((at & first) | (at2 & second), 1.0, rows[q0])
            for block in wide[c + 2 :] + [rows]:
                a, b = subs(block[q0], s), subs(block[q0], s + 1)
                for q in range(h):
                    block[q] = block[q] - (left[q] * a + right[q] * b)
        even = (sub & 1) == 0
        swapped = [jnp.where(even, pltpu.roll(rows[q], 7, 0), pltpu.roll(rows[q], 1, 0)) for q in range(h)]
        rows = [rows[q] * unscaled[0][q] - swapped[q] * unscaled[1][q] for q in range(h)]
        w = [subs(rows[c // 8], c % 8) for c in range(width)]
        keep = (lane < base) | (lane >= base + width)
        near = list(range(m + h, min(m + 2 * h, n)))
        far = [i for i in list(range(m + 2 * h, n)) + list(range(m))]
        for i in near:
            t = [lanes(tiles[i], base + c) * w[c] for c in range(width)]
            while len(t) > 1:
                t = [a + b for a, b in zip(t[::2], t[1::2])]
            tiles[i] = jnp.where(keep, tiles[i], 0.0) - t[0]
        padded = jnp.concatenate([rows[i - m] if m <= i < m + h else blank for i in range(n)], 0)
        change = dot(jnp.concatenate([tiles[i] for i in far], 0), padded)
        for j, i in enumerate(far):
            tiles[i] = jnp.where(keep, tiles[i], 0.0) - change[8 * j : 8 * j + 8]
        tiles[m : m + h] = rows
    return tiles


def solve_kernel(size, pieces, damp_ref, *refs):
    nb = size // B
    got, x_ref, (pack_ref, d_ref, v_ref, *panels) = refs[: 2 * pieces], refs[2 * pieces], refs[2 * pieces + 1 :]
    w_refs, z_refs = panels[:nb], panels[nb:]
    piece = got[0].shape[0]
    spots = [piece_rows(t, own, piece * pieces, piece) for own in (True, False) for t in range(pieces)]
    for ref, rows in zip(got, spots):
        pack_ref[rows, :] = ref[...]
    starts = panel_starts(size)
    factor = damp_ref[0]
    zero = jnp.minimum(jnp.full((8, B), jnp.abs(factor)), 0.0)
    lane = lax.broadcasted_iota(jnp.int32, (8, B), 1)
    sub = lax.broadcasted_iota(jnp.int32, (8, B), 0)
    for k, w_ref in enumerate(w_refs):
        rows = size - k * B
        w_ref[0:rows, :] = pack_ref[starts[k] : starts[k + 1], :]
        w_ref[rows : rows + 8, :] = jnp.broadcast_to(pack_ref[starts[-1] + k : starts[-1] + k + 1, :], (8, B))
        for t in range(B // 8):
            a = w_ref[8 * t : 8 * t + 8, :]
            w_ref[8 * t : 8 * t + 8, :] = a + jnp.where(lane == sub + 8 * t, a * factor, 0.0)
    d_ref[...] = w_refs[0][0:B, :]

    def step(i, carry):
        inv = inverse([d_ref[8 * t : 8 * t + 8, :] for t in range(B // 8)], zero)
        for t in range(B // 8):
            v_ref[8 * t : 8 * t + 8, :] = inv[t]
        for k in range(nb):

            @pl.when(i == k)
            def _():
                z_refs[k][...] = dot(w_refs[k][B:, :], v_ref[...])
                for j in range(k + 1, nb):
                    at = (j - k) * B
                    new = w_refs[j][...] - dot(
                        z_refs[k][at - B :, :], w_refs[k][at : at + B, :], ((1,), (1,))
                    )
                    if j == k + 1:
                        d_ref[...] = new[0:B]
                    w_refs[j][...] = new

        return carry

    lax.fori_loop(0, nb, step, 0)
    x = [None] * nb
    for k in reversed(range(nb)):
        below = (nb - 1 - k) * B
        s = z_refs[k][below : below + 8, :]
        for j in range(k + 1, nb):
            s = s - dot(x[j], z_refs[k][(j - k - 1) * B : (j - k) * B, :])
        x[k] = s
        x_ref[0:1, k * B : (k + 1) * B] = -s[0:1]


def solve_call(size, total, damping, got):
    nb = size // B
    scratch = lambda rows: pltpu.VMEM((rows, B), jnp.float32)
    return pl.pallas_call(
        functools.partial(solve_kernel, size, len(got) // 2),
        out_shape=f32(1, size),
        in_specs=[SMEM] + [VMEM] * len(got),
        out_specs=VMEM,
        scratch_shapes=[scratch(total), scratch(B), scratch(B)]
        + [scratch(size - k * B + 8) for k in range(nb)]
        + [scratch(size - (k + 1) * B + 8) for k in range(nb)],
        compiler_params=pltpu.CompilerParams(vmem_limit_bytes=KERNEL_VMEM),
        name="solve",
    )(damping, *got)


def tree_sum(parts):
    while len(parts) > 1:
        parts = [a + b for a, b in zip(parts[::2], parts[1::2])]
    return parts[0]


def per_device(jacobian, residual, damping):
    sensors, spaces = lax.axis_size("sensor"), lax.axis_size("space")
    part, seen = jacobian.shape
    size = part * spaces
    span = seen // spaces
    me = lax.axis_index("space")
    both = ("sensor", "space")

    def swap(x, bits):
        return lax.ppermute(x, both, [(i, i ^ bits) for i in range(sensors * spaces)])

    def panel(step):
        return lax.dynamic_slice_in_dim(jacobian, (me ^ step) * span, span, 1)

    far = list(range(spaces - 1, spaces // 2 - 1, -1))
    order = far[1::2] + list(range(2, spaces // 2)) + far[::2] + [1]
    got = [swap(panel(step), step) for step in order]
    seen_residual = lax.dynamic_slice_in_dim(residual, me * span, span, 0).reshape(1, span)

    blocks = panel_starts(size)[-1]
    unit = 16 * sensors
    total = -(-(blocks + size // B) // unit) * unit
    pieces = sensors
    piece = total // 2 // pieces
    packed = pl.pallas_call(
        functools.partial(gram_kernel, order, total, pieces),
        out_shape=[f32(piece, B)] * (2 * pieces),
        in_specs=[VMEM] * (spaces + 1),
        out_specs=[VMEM] * (2 * pieces),
        scratch_shapes=[
            pltpu.VMEM((size, span), jnp.float32),
            pltpu.VMEM((total, B), jnp.float32),
        ],
        compiler_params=pltpu.CompilerParams(vmem_limit_bytes=KERNEL_VMEM),
        name="gram",
    )(seen_residual, panel(0), *got)
    plane = [(t >> 1) * 2 * spaces + (t & 1) for t in range(pieces)]
    sums = [kept + swap(sent, spaces) for sent, kept in zip(packed[:pieces], packed[pieces:])]
    mine = tree_sum([sums[0]] + [swap(sums[t], plane[t]) for t in range(1, pieces)])
    mine = tree_sum([mine] + [swap(mine, 2 * u) for u in range(1, spaces // 2)])
    half = [mine] + [swap(mine, plane[t]) for t in range(1, pieces)]
    x = solve_call(size, total, damping, half + [swap(x, spaces) for x in half])
    return x.reshape(size)


def solution(mesh):
    placed = (P("space", "sensor"), P("sensor"), P())
    return jax.shard_map(per_device, mesh=mesh, in_specs=placed, out_specs=P(), check_vma=False)
```

```python
import functools

import jax
import jax.numpy as jnp
from jax import lax
from jax.experimental import pallas as pl
from jax.experimental.pallas import tpu as pltpu
from jax.sharding import PartitionSpec as P

B = 128
VMEM = pl.BlockSpec(memory_space=pltpu.VMEM)
SMEM = pl.BlockSpec(memory_space=pltpu.SMEM)
ANY = pl.BlockSpec(memory_space=pl.ANY)
KERNEL_VMEM = 16 << 20


def f32(*shape):
    return jax.ShapeDtypeStruct(shape, jnp.float32)


def dot(a, b, dims=((1,), (0,))):
    return lax.dot_general(
        a, b, (dims, ((), ())), precision=lax.Precision.HIGHEST, preferred_element_type=jnp.float32
    )


def panel_starts(size):
    starts = [0]
    for k in range(size // B):
        starts.append(starts[-1] + size - k * B)
    return starts


def plane_index():
    return lax.div(lax.axis_index("sensor"), 2) * 2 + lax.rem(lax.axis_index("space"), 2)


def piece_rows(t, own, half, piece):
    core = lax.rem(lax.axis_index("sensor"), 2)
    side = core if own else 1 - core
    return pl.ds(pl.multiple_of(side * half + jnp.bitwise_xor(plane_index(), t) * piece, 8), piece)


def gram_kernel(order, total, pieces, *refs):
    n = len(order)
    residual_ref, own_ref, *got = refs[: n + 2]
    outs = refs[n + 2 : n + 2 + 2 * pieces]
    rows_ref, pack_ref = refs[n + 2 + 2 * pieces :]
    me = lax.axis_index("space")
    size, span = rows_ref.shape
    part = own_ref.shape[0]
    for step, ref in zip([0] + order, [own_ref] + got):
        rows_ref[pl.ds(pl.multiple_of(jnp.bitwise_xor(me, step) * part, part), part), :] = ref[...]
    starts = panel_starts(size)
    wide = 2 * B if size % (2 * B) == 0 else B
    for lo in range(0, size, wide):
        gram = dot(rows_ref[lo:, :], rows_ref[lo : lo + wide, :], ((1,), (1,)))
        for skip in range(0, wide, B):
            k = (lo + skip) // B
            pack_ref[starts[k] : starts[k + 1], :] = gram[skip:, skip : skip + B]
    grad = dot(jnp.broadcast_to(residual_ref[...], (8, span)), rows_ref[...], ((1,), (1,)))
    tail = starts[-1]
    pack_ref[tail:total, :] = jnp.zeros((total - tail, B), jnp.float32)
    for k in range(size // B):
        pack_ref[tail + k : tail + k + 1, :] = grad[0:1, k * B : (k + 1) * B]
    half = total // 2
    piece = half // pieces
    spots = [piece_rows(t, own, half, piece) for own in (False, True) for t in range(pieces)]
    for rows, out in zip(spots, outs):
        out[...] = pack_ref[rows, :]


def lanes(x, l):
    return jnp.broadcast_to(x[:, l : l + 1], x.shape)


def subs(x, s):
    return jnp.broadcast_to(x[s : s + 1, :], x.shape)


def inverse(tiles, zero, chores=(), width=16):
    tiles = list(tiles)
    n, h = len(tiles), width // 8
    lane = lax.broadcasted_iota(jnp.int32, tiles[0].shape, 1)
    sub = lax.broadcasted_iota(jnp.int32, tiles[0].shape, 0)
    blank = jnp.zeros_like(tiles[0])
    for m in range(0, n, h):
        base = 8 * m
        rows = tiles[m : m + h]
        wide = [[lanes(rows[q], base + c) for q in range(h)] for c in range(width)]
        wide = [[column[0] + zero] + column[1:] for column in wide]
        keep = (lane < base) | (lane >= base + width)
        rows = [jnp.where(keep, rows[q], jnp.where(lane == sub + base + 8 * q, 1.0, 0.0)) for q in range(h)]
        unscaled = [[blank] * h, [blank] * h]
        for c in range(0, width, 2):
            q0, s = divmod(c, 8)
            first = sub == s
            pair = first | (sub == s + 1)
            one, two = wide[c], wide[c + 1]
            p11, p21, p22 = subs(one[q0], s), subs(one[q0], s + 1), subs(two[q0], s + 1)
            inv = 1.0 / (p11 * p22 - p21 * p21)
            left = [(one[q] * p22 - two[q] * p21) * inv for q in range(h)]
            right = [(two[q] * p11 - one[q] * p21) * inv for q in range(h)]
            left[q0], right[q0] = jnp.where(pair, 0.0, left[q0]), jnp.where(pair, 0.0, right[q0])
            unscaled[0][q0] = jnp.where(pair, jnp.where(first, p22, p11) * inv, unscaled[0][q0])
            unscaled[1][q0] = jnp.where(pair, p21 * inv, unscaled[1][q0])
            for block in wide[c + 2 :] + [rows]:
                a, b = subs(block[q0], s), subs(block[q0], s + 1)
                for q in range(h):
                    block[q] = block[q] - (left[q] * a + right[q] * b)
        even = (sub & 1) == 0
        swapped = [jnp.where(even, pltpu.roll(rows[q], 7, 0), pltpu.roll(rows[q], 1, 0)) for q in range(h)]
        rows = [rows[q] * unscaled[0][q] - swapped[q] * unscaled[1][q] for q in range(h)]
        w = [subs(rows[c // 8], c % 8) for c in range(width)]
        near = list(range(m + h, min(m + 2 * h, n)))
        far = [i for i in list(range(m + 2 * h, n)) + list(range(m))]
        for i in near:
            t = [lanes(tiles[i], base + c) * w[c] for c in range(width)]
            while len(t) > 1:
                t = [a + b for a, b in zip(t[::2], t[1::2])]
            tiles[i] = jnp.where(keep, tiles[i], 0.0) - t[0]
        padded = jnp.concatenate([rows[i - m] if m <= i < m + h else blank for i in range(n)], 0)
        change = dot(jnp.concatenate([tiles[i] for i in far], 0), padded)
        for j, i in enumerate(far):
            tiles[i] = jnp.where(keep, tiles[i], 0.0) - change[8 * j : 8 * j + 8]
        tiles[m : m + h] = rows
        share = -(-len(chores) // (n // h - 1))
        for chore in chores[m // h * share : (m // h + 1) * share]:
            chore()
    return tiles


def solve_kernel(size, pieces, damp_ref, *refs):
    nb = size // B
    got, x_ref, (pack_ref, v_ref, *panels) = refs[: 2 * pieces], refs[2 * pieces], refs[2 * pieces + 1 :]
    w_refs, z_refs = panels[:nb], panels[nb:]
    piece = got[0].shape[0]
    spots = [piece_rows(t, own, piece * pieces, piece) for own in (True, False) for t in range(pieces)]
    for ref, rows in zip(got, spots):
        pack_ref[rows, :] = ref[...]
    starts = panel_starts(size)
    factor = damp_ref[0]
    zero = jnp.minimum(jnp.full((8, B), jnp.abs(factor)), 0.0)
    lane = lax.broadcasted_iota(jnp.int32, (8, B), 1)
    sub = lax.broadcasted_iota(jnp.int32, (8, B), 0)
    for k, w_ref in enumerate(w_refs):
        rows = size - k * B
        w_ref[0:rows, :] = pack_ref[starts[k] : starts[k + 1], :]
        w_ref[rows : rows + 8, :] = jnp.broadcast_to(pack_ref[starts[-1] + k : starts[-1] + k + 1, :], (8, B))
        for t in range(B // 8):
            a = w_ref[8 * t : 8 * t + 8, :]
            w_ref[8 * t : 8 * t + 8, :] = a + jnp.where(lane == sub + 8 * t, a * factor, 0.0)
    def scale(k, lo, hi):
        z_refs[k][lo:hi, :] = dot(w_refs[k][B + lo : B + hi, :], v_ref[k * B : (k + 1) * B, :])

    def update(k, j, lo, hi):
        at = (j - k) * B
        z = z_refs[k][at - B + lo : at - B + hi, :]
        w_refs[j][lo:hi, :] -= dot(z, w_refs[k][at : at + B, :], ((1,), (1,)))

    chores = []
    for k in range(nb):
        inv = inverse([w_refs[k][8 * t : 8 * t + 8, :] for t in range(B // 8)], zero, chores)
        for t in range(B // 8):
            v_ref[k * B + 8 * t : k * B + 8 * t + 8, :] = inv[t]
        below = size - (k + 1) * B
        if below:
            scale(k, 0, B)
            update(k, k + 1, 0, B)
        cuts = list(range(B if below else 0, below, B)) + [below]
        chores = [functools.partial(scale, k, lo, min(lo + B, below) if lo < below else below + 8) for lo in cuts]
        for j in range(k + 1, nb):
            rows = size - j * B
            for lo in range(B if j == k + 1 else 0, rows + 8, B):
                chores.append(functools.partial(update, k, j, lo, min(lo + B, rows) if lo < rows else rows + 8))
    for chore in chores:
        chore()
    x = [None] * nb
    for k in reversed(range(nb)):
        below = (nb - 1 - k) * B
        s = z_refs[k][below : below + 8, :]
        for j in range(k + 1, nb):
            s = s - dot(x[j], z_refs[k][(j - k - 1) * B : (j - k) * B, :])
        x[k] = s
        x_ref[0:1, k * B : (k + 1) * B] = -s[0:1]


def solve_call(size, total, damping, got):
    nb = size // B
    scratch = lambda rows: pltpu.VMEM((rows, B), jnp.float32)
    return pl.pallas_call(
        functools.partial(solve_kernel, size, len(got) // 2),
        out_shape=f32(1, size),
        in_specs=[SMEM] + [VMEM] * len(got),
        out_specs=VMEM,
        scratch_shapes=[scratch(total), scratch(size)]
        + [scratch(size - k * B + 8) for k in range(nb)]
        + [scratch(size - (k + 1) * B + 8) for k in range(nb)],
        compiler_params=pltpu.CompilerParams(vmem_limit_bytes=KERNEL_VMEM),
        name="solve",
    )(damping, *got)


def tree_sum(parts):
    while len(parts) > 1:
        parts = [a + b for a, b in zip(parts[::2], parts[1::2])]
    return parts[0]


def per_device(jacobian, residual, damping):
    sensors, spaces = lax.axis_size("sensor"), lax.axis_size("space")
    part, seen = jacobian.shape
    size = part * spaces
    span = seen // spaces
    me = lax.axis_index("space")
    both = ("sensor", "space")

    def swap(x, bits):
        return lax.ppermute(x, both, [(i, i ^ bits) for i in range(sensors * spaces)])

    def panel(step):
        return lax.dynamic_slice_in_dim(jacobian, (me ^ step) * span, span, 1)

    far = list(range(spaces - 1, spaces // 2 - 1, -1))
    order = far[1::2] + list(range(2, spaces // 2)) + far[::2] + [1]
    got = [swap(panel(step), step) for step in order]
    seen_residual = lax.dynamic_slice_in_dim(residual, me * span, span, 0).reshape(1, span)

    blocks = panel_starts(size)[-1]
    unit = 16 * sensors
    total = -(-(blocks + size // B) // unit) * unit
    pieces = sensors
    piece = total // 2 // pieces
    packed = pl.pallas_call(
        functools.partial(gram_kernel, order, total, pieces),
        out_shape=[f32(piece, B)] * (2 * pieces),
        in_specs=[VMEM] * (spaces + 1),
        out_specs=[VMEM] * (2 * pieces),
        scratch_shapes=[
            pltpu.VMEM((size, span), jnp.float32),
            pltpu.VMEM((total, B), jnp.float32),
        ],
        compiler_params=pltpu.CompilerParams(vmem_limit_bytes=KERNEL_VMEM),
        name="gram",
    )(seen_residual, panel(0), *got)
    plane = [(t >> 1) * 2 * spaces + (t & 1) for t in range(pieces)]
    sums = [kept + swap(sent, spaces) for sent, kept in zip(packed[:pieces], packed[pieces:])]
    mine = tree_sum([sums[0]] + [swap(sums[t], plane[t]) for t in range(1, pieces)])
    mine = tree_sum([mine] + [swap(mine, 2 * u) for u in range(1, spaces // 2)])
    half = [mine] + [swap(mine, plane[t]) for t in range(1, pieces)]
    x = solve_call(size, total, damping, half + [swap(x, spaces) for x in half])
    return x.reshape(size)


def solution(mesh):
    placed = (P("space", "sensor"), P("sensor"), P())
    return jax.shard_map(per_device, mesh=mesh, in_specs=placed, out_specs=P(), check_vma=False)
```

```python
import functools

import jax
import jax.numpy as jnp
from jax import lax
from jax.experimental import pallas as pl
from jax.experimental.pallas import tpu as pltpu
from jax.sharding import PartitionSpec as P


B = 128
VMEM = pl.BlockSpec(memory_space=pltpu.VMEM)
SMEM = pl.BlockSpec(memory_space=pltpu.SMEM)
ANY = pl.BlockSpec(memory_space=pl.ANY)
KERNEL_VMEM = 16 << 20


def f32(*shape):
    return jax.ShapeDtypeStruct(shape, jnp.float32)


def dot(a, b, dims=((1,), (0,))):
    return lax.dot_general(
        a, b, (dims, ((), ())), precision=lax.Precision.HIGHEST, preferred_element_type=jnp.float32
    )


def panel_starts(size):
    starts = [0]
    for k in range(size // B):
        starts.append(starts[-1] + size - k * B)
    return starts


def plane_index():
    return lax.div(lax.axis_index("sensor"), 2) * 2 + lax.rem(lax.axis_index("space"), 2)


def piece_rows(t, own, half, piece):
    core = lax.rem(lax.axis_index("sensor"), 2)
    side = core if own else 1 - core
    return pl.ds(pl.multiple_of(side * half + jnp.bitwise_xor(plane_index(), t) * piece, 8), piece)


def gram_kernel(order, total, pieces, *refs):
    n = len(order)
    residual_ref, own_ref, *got = refs[: n + 2]
    outs = refs[n + 2 : n + 2 + 2 * pieces]
    rows_ref, pack_ref = refs[n + 2 + 2 * pieces :]
    me = lax.axis_index("space")
    size, span = rows_ref.shape
    part = own_ref.shape[0]
    for step, ref in zip([0] + order, [own_ref] + got):
        rows_ref[pl.ds(pl.multiple_of(jnp.bitwise_xor(me, step) * part, part), part), :] = ref[...]
    starts = panel_starts(size)
    wide = 2 * B if size % (2 * B) == 0 else B
    for lo in range(0, size, wide):
        gram = dot(rows_ref[lo:, :], rows_ref[lo : lo + wide, :], ((1,), (1,)))
        for skip in range(0, wide, B):
            k = (lo + skip) // B
            pack_ref[starts[k] : starts[k + 1], :] = gram[skip:, skip : skip + B]
    grad = dot(jnp.broadcast_to(residual_ref[...], (8, span)), rows_ref[...], ((1,), (1,)))
    for i in range(2 * size // B):
        row = starts[-2] + i
        pack_ref[row : row + 1, B // 2 :] = grad[0:1, i * (B // 2) : (i + 1) * (B // 2)]
    if total > starts[-1]:
        pack_ref[starts[-1] : total, :] = jnp.zeros((total - starts[-1], B), jnp.float32)
    half = total // 2
    piece = half // pieces
    spots = [piece_rows(t, own, half, piece) for own in (False, True) for t in range(pieces)]
    for rows, out in zip(spots, outs):
        out[...] = pack_ref[rows, :]


def lanes(x, l):
    return jnp.broadcast_to(x[:, l : l + 1], x.shape)


def subs(x, s):
    return jnp.broadcast_to(x[s : s + 1, :], x.shape)


def inverse(tiles, zero, chores=(), width=16):
    tiles = list(tiles)
    n, h = len(tiles), width // 8
    lane = lax.broadcasted_iota(jnp.int32, tiles[0].shape, 1)
    sub = lax.broadcasted_iota(jnp.int32, tiles[0].shape, 0)
    blank = jnp.zeros_like(tiles[0])
    for m in range(0, n, h):
        base = 8 * m
        rows = tiles[m : m + h]
        wide = [[lanes(rows[q], base + c) for q in range(h)] for c in range(width)]
        wide = [[column[0] + zero] + column[1:] for column in wide]
        keep = (lane < base) | (lane >= base + width)
        rows = [jnp.where(keep, rows[q], jnp.where(lane == sub + base + 8 * q, 1.0, 0.0)) for q in range(h)]
        unscaled = [[blank] * h, [blank] * h]
        for c in range(0, width, 2):
            q0, s = divmod(c, 8)
            first = sub == s
            pair = first | (sub == s + 1)
            one, two = wide[c], wide[c + 1]
            p11, p21, p22 = subs(one[q0], s), subs(one[q0], s + 1), subs(two[q0], s + 1)
            inv = 1.0 / (p11 * p22 - p21 * p21)
            left = [(one[q] * p22 - two[q] * p21) * inv for q in range(h)]
            right = [(two[q] * p11 - one[q] * p21) * inv for q in range(h)]
            left[q0], right[q0] = jnp.where(pair, 0.0, left[q0]), jnp.where(pair, 0.0, right[q0])
            unscaled[0][q0] = jnp.where(pair, jnp.where(first, p22, p11) * inv, unscaled[0][q0])
            unscaled[1][q0] = jnp.where(pair, p21 * inv, unscaled[1][q0])
            for block in wide[c + 2 :] + [rows]:
                a, b = subs(block[q0], s), subs(block[q0], s + 1)
                for q in range(h):
                    block[q] = block[q] - (left[q] * a + right[q] * b)
        even = (sub & 1) == 0
        swapped = [jnp.where(even, pltpu.roll(rows[q], 7, 0), pltpu.roll(rows[q], 1, 0)) for q in range(h)]
        rows = [rows[q] * unscaled[0][q] - swapped[q] * unscaled[1][q] for q in range(h)]
        w = [subs(rows[c // 8], c % 8) for c in range(width)]
        near = list(range(m + h, min(m + 2 * h, n)))
        far = [i for i in list(range(m + 2 * h, n)) + list(range(m))]
        for i in near:
            t = [lanes(tiles[i], base + c) * w[c] for c in range(width)]
            while len(t) > 1:
                t = [a + b for a, b in zip(t[::2], t[1::2])]
            tiles[i] = jnp.where(keep, tiles[i], 0.0) - t[0]
        padded = jnp.concatenate([rows[i - m] if m <= i < m + h else blank for i in range(n)], 0)
        change = dot(jnp.concatenate([tiles[i] for i in far], 0), padded)
        for j, i in enumerate(far):
            tiles[i] = jnp.where(keep, tiles[i], 0.0) - change[8 * j : 8 * j + 8]
        tiles[m : m + h] = rows
        share = -(-len(chores) // (n // h - 1))
        for chore in chores[m // h * share : (m // h + 1) * share]:
            chore()
    return tiles


def solve_kernel(size, pieces, damp_ref, *refs):
    nb = size // B
    got, x_ref, (pack_ref, v_ref, *panels) = refs[: 2 * pieces], refs[2 * pieces], refs[2 * pieces + 1 :]
    w_refs, z_refs = panels[:nb], panels[nb:]
    piece = got[0].shape[0]
    spots = [piece_rows(t, own, piece * pieces, piece) for own in (True, False) for t in range(pieces)]
    for ref, rows in zip(got, spots):
        pack_ref[rows, :] = ref[...]
    starts = panel_starts(size)
    factor = damp_ref[0]
    zero = jnp.minimum(jnp.full((8, B), jnp.abs(factor)), 0.0)
    lane = lax.broadcasted_iota(jnp.int32, (8, B), 1)
    sub = lax.broadcasted_iota(jnp.int32, (8, B), 0)
    for k, w_ref in enumerate(w_refs):
        rows = size - k * B
        w_ref[0:rows, :] = pack_ref[starts[k] : starts[k + 1], :]
        for side in (0, 1):
            at = starts[-2] + 2 * k + side
            w_ref[rows : rows + 8, side * (B // 2) : (side + 1) * (B // 2)] = jnp.broadcast_to(
                pack_ref[at : at + 1, B // 2 :], (8, B // 2)
            )
        if k == nb - 1:
            w_ref[0 : 2 * nb, B // 2 : B] = w_ref[B // 2 : B, :].T[0 : 2 * nb, :]
        for t in range(B // 8):
            a = w_ref[8 * t : 8 * t + 8, :]
            w_ref[8 * t : 8 * t + 8, :] = a + jnp.where(lane == sub + 8 * t, a * factor, 0.0)

    def scale(k, lo, hi):
        z_refs[k][lo:hi, :] = dot(w_refs[k][B + lo : B + hi, :], v_ref[k * B : (k + 1) * B, :])

    def update(k, j, lo, hi):
        at = (j - k) * B
        z = z_refs[k][at - B + lo : at - B + hi, :]
        w_refs[j][lo:hi, :] -= dot(z, w_refs[k][at : at + B, :], ((1,), (1,)))

    chores = []
    for k in range(nb):
        inv = inverse([w_refs[k][8 * t : 8 * t + 8, :] for t in range(B // 8)], zero, chores)
        for t in range(B // 8):
            v_ref[k * B + 8 * t : k * B + 8 * t + 8, :] = inv[t]
        below = size - (k + 1) * B
        if below:
            scale(k, 0, B)
            update(k, k + 1, 0, B)
        cuts = list(range(B if below else 0, below, B)) + [below]
        chores = [functools.partial(scale, k, lo, min(lo + B, below) if lo < below else below + 8) for lo in cuts]
        for j in range(k + 1, nb):
            rows = size - j * B
            for lo in range(B if j == k + 1 else 0, rows + 8, B):
                chores.append(functools.partial(update, k, j, lo, min(lo + B, rows) if lo < rows else rows + 8))
    for chore in chores:
        chore()
    x = [None] * nb
    for k in reversed(range(nb)):
        below = (nb - 1 - k) * B
        s = z_refs[k][below : below + 8, :]
        for j in range(k + 1, nb):
            s = s - dot(x[j], z_refs[k][(j - k - 1) * B : (j - k) * B, :])
        x[k] = s
        x_ref[0:1, k * B : (k + 1) * B] = -s[0:1]


def solve_call(size, total, damping, got):
    nb = size // B
    scratch = lambda rows: pltpu.VMEM((rows, B), jnp.float32)
    return pl.pallas_call(
        functools.partial(solve_kernel, size, len(got) // 2),
        out_shape=f32(1, size),
        in_specs=[SMEM] + [VMEM] * len(got),
        out_specs=VMEM,
        scratch_shapes=[scratch(total), scratch(size)]
        + [scratch(size - k * B + 8) for k in range(nb)]
        + [scratch(size - (k + 1) * B + 8) for k in range(nb)],
        compiler_params=pltpu.CompilerParams(vmem_limit_bytes=KERNEL_VMEM),
        name="solve",
    )(damping, *got)


def tree_sum(parts):
    while len(parts) > 1:
        parts = [a + b for a, b in zip(parts[::2], parts[1::2])]
    return parts[0]


def per_device(jacobian, residual, damping):
    sensors, spaces = lax.axis_size("sensor"), lax.axis_size("space")
    part, seen = jacobian.shape
    size = part * spaces
    span = seen // spaces
    me = lax.axis_index("space")
    both = ("sensor", "space")

    def swap(x, bits):
        return lax.ppermute(x, both, [(i, i ^ bits) for i in range(sensors * spaces)])

    def panel(step):
        return lax.dynamic_slice_in_dim(jacobian, (me ^ step) * span, span, 1)

    far = list(range(spaces - 1, spaces // 2 - 1, -1))
    order = far[1::2] + list(range(2, spaces // 2)) + far[::2] + [1]
    first = panel(order[0])
    jacobian, first = lax.optimization_barrier((jacobian, first))
    got = [swap(first, order[0])]
    late = [panel(step) for step in [0] + order[1:]]
    got += [swap(x, step) for x, step in zip(late[1:], order[1:])]
    seen_residual = lax.dynamic_slice_in_dim(residual, me * span, span, 0).reshape(1, span)

    blocks = panel_starts(size)[-1]
    unit = 16 * sensors
    total = -(-blocks // unit) * unit
    pieces = sensors
    piece = total // 2 // pieces
    packed = pl.pallas_call(
        functools.partial(gram_kernel, order, total, pieces),
        out_shape=[f32(piece, B)] * (2 * pieces),
        in_specs=[VMEM] * (spaces + 1),
        out_specs=[VMEM] * (2 * pieces),
        scratch_shapes=[
            pltpu.VMEM((size, span), jnp.float32),
            pltpu.VMEM((total, B), jnp.float32),
        ],
        compiler_params=pltpu.CompilerParams(vmem_limit_bytes=KERNEL_VMEM),
        name="gram",
    )(seen_residual, late[0], *got)
    plane = [(t >> 1) * 2 * spaces + (t & 1) for t in range(pieces)]
    sums = [kept + swap(sent, spaces) for sent, kept in zip(packed[:pieces], packed[pieces:])]
    mine = tree_sum([sums[0]] + [swap(sums[t], plane[t]) for t in range(1, pieces)])
    mine = tree_sum([mine] + [swap(mine, 2 * u) for u in range(1, spaces // 2)])
    half = [mine] + [swap(mine, plane[t]) for t in range(1, pieces)]
    x = solve_call(size, total, damping, half + [swap(x, spaces) for x in half])
    return x.reshape(size)


def solution(mesh):
    placed = (P("space", "sensor"), P("sensor"), P())
    return jax.shard_map(per_device, mesh=mesh, in_specs=placed, out_specs=P(), check_vma=False)
```

```python
import functools

import jax
import jax.numpy as jnp
from jax import lax
from jax.experimental import pallas as pl
from jax.experimental.pallas import tpu as pltpu
from jax.sharding import PartitionSpec as P


B = 128
VMEM = pl.BlockSpec(memory_space=pltpu.VMEM)
SMEM = pl.BlockSpec(memory_space=pltpu.SMEM)
ANY = pl.BlockSpec(memory_space=pl.ANY)
KERNEL_VMEM = 16 << 20


def f32(*shape):
    return jax.ShapeDtypeStruct(shape, jnp.float32)


def dot(a, b, dims=((1,), (0,))):
    return lax.dot_general(
        a, b, (dims, ((), ())), precision=lax.Precision.HIGHEST, preferred_element_type=jnp.float32
    )


def panel_starts(size):
    starts = [0]
    for k in range(size // B):
        starts.append(starts[-1] + size - k * B)
    return starts


def plane_index():
    return lax.div(lax.axis_index("sensor"), 2) * 2 + lax.rem(lax.axis_index("space"), 2)


def piece_rows(t, own, half, piece):
    core = lax.rem(lax.axis_index("sensor"), 2)
    side = core if own else 1 - core
    return pl.ds(pl.multiple_of(side * half + jnp.bitwise_xor(plane_index(), t) * piece, 8), piece)


def gather_rows(first, steps, refs, rows_ref):
    part = refs[0].shape[0]
    for step, ref in zip(steps, refs):
        at = (jnp.bitwise_xor(lax.axis_index("space"), step) - first) * part
        rows_ref[pl.ds(pl.multiple_of(at, 8), part), :] = ref[...]


def gradient(residual_ref, rows_ref):
    residual = jnp.broadcast_to(residual_ref[...], (8, residual_ref.shape[1]))
    return dot(residual, rows_ref[...], ((1,), (1,)))


def near_kernel(spaces, residual_ref, *refs):
    *got, rows_ref, products_ref, grad_ref = refs
    half = spaces // 2
    first = lax.div(lax.axis_index("space"), half) * half
    gather_rows(first, range(half), got, rows_ref)
    products_ref[...] = dot(rows_ref[...], rows_ref[...], ((1,), (1,)))
    grad_ref[...] = gradient(residual_ref, rows_ref)


def gram_kernel(order, total, pieces, residual_ref, near_ref, products_ref, grad_ref, *refs):
    got, outs, (rows_ref, pack_ref) = refs[: len(order)], refs[len(order) : -2], refs[-2:]
    spaces = 2 * len(order)
    cut = rows_ref.shape[0]
    size = 2 * cut
    starts = panel_starts(size)
    side = lax.div(lax.axis_index("space"), spaces // 2)
    gather_rows((1 - side) * (spaces // 2), order, got, rows_ref)
    products = dot(rows_ref[...], rows_ref[...], ((1,), (1,)))
    grad = gradient(residual_ref, rows_ref)

    def put(low, high, cross, grads):
        for k in range(size // B):
            own = low if k * B < cut else high
            lo = k * B % cut
            pack_ref[starts[k] : starts[k] + cut - lo, :] = own[lo:, lo : lo + B]
            if k * B < cut:
                pack_ref[starts[k] + cut - lo : starts[k + 1], :] = cross[:, lo : lo + B]
        for i in range(2 * size // B):
            row, at = starts[-2] + i, i * (B // 2)
            pack_ref[row : row + 1, B // 2 :] = grads[at // cut][0:1, at % cut : at % cut + B // 2]

    @pl.when(side == 0)
    def _():
        cross = dot(rows_ref[...], near_ref[...], ((1,), (1,)))
        put(products_ref, products, cross, (grad_ref, grad))

    @pl.when(side == 1)
    def _():
        cross = dot(near_ref[...], rows_ref[...], ((1,), (1,)))
        put(products, products_ref, cross, (grad, grad_ref))

    if total > starts[-1]:
        pack_ref[starts[-1] : total, :] = jnp.zeros((total - starts[-1], B), jnp.float32)
    half = total // 2
    piece = half // pieces
    spots = [piece_rows(t, own, half, piece) for own in (False, True) for t in range(pieces)]
    for rows, out in zip(spots, outs):
        out[...] = pack_ref[rows, :]


def lanes(x, l):
    return jnp.broadcast_to(x[:, l : l + 1], x.shape)


def subs(x, s):
    return jnp.broadcast_to(x[s : s + 1, :], x.shape)


def inverse(tiles, zero, chores=(), width=16):
    tiles = list(tiles)
    n, h = len(tiles), width // 8
    lane = lax.broadcasted_iota(jnp.int32, tiles[0].shape, 1)
    sub = lax.broadcasted_iota(jnp.int32, tiles[0].shape, 0)
    blank = jnp.zeros_like(tiles[0])
    for m in range(0, n, h):
        base = 8 * m
        rows = tiles[m : m + h]
        wide = [[lanes(rows[q], base + c) for q in range(h)] for c in range(width)]
        wide = [[column[0] + zero] + column[1:] for column in wide]
        keep = (lane < base) | (lane >= base + width)
        rows = [jnp.where(keep, rows[q], jnp.where(lane == sub + base + 8 * q, 1.0, 0.0)) for q in range(h)]
        unscaled = [[blank] * h, [blank] * h]
        for c in range(0, width, 2):
            q0, s = divmod(c, 8)
            first = sub == s
            pair = first | (sub == s + 1)
            one, two = wide[c], wide[c + 1]
            p11, p21, p22 = subs(one[q0], s), subs(one[q0], s + 1), subs(two[q0], s + 1)
            inv = 1.0 / (p11 * p22 - p21 * p21)
            left = [(one[q] * p22 - two[q] * p21) * inv for q in range(h)]
            right = [(two[q] * p11 - one[q] * p21) * inv for q in range(h)]
            left[q0], right[q0] = jnp.where(pair, 0.0, left[q0]), jnp.where(pair, 0.0, right[q0])
            unscaled[0][q0] = jnp.where(pair, jnp.where(first, p22, p11) * inv, unscaled[0][q0])
            unscaled[1][q0] = jnp.where(pair, p21 * inv, unscaled[1][q0])
            for block in wide[c + 2 :] + [rows]:
                a, b = subs(block[q0], s), subs(block[q0], s + 1)
                for q in range(h):
                    block[q] = block[q] - (left[q] * a + right[q] * b)
        even = (sub & 1) == 0
        swapped = [jnp.where(even, pltpu.roll(rows[q], 7, 0), pltpu.roll(rows[q], 1, 0)) for q in range(h)]
        rows = [rows[q] * unscaled[0][q] - swapped[q] * unscaled[1][q] for q in range(h)]
        w = [subs(rows[c // 8], c % 8) for c in range(width)]
        near = list(range(m + h, min(m + 2 * h, n)))
        far = [i for i in list(range(m + 2 * h, n)) + list(range(m))]
        for i in near:
            t = [lanes(tiles[i], base + c) * w[c] for c in range(width)]
            while len(t) > 1:
                t = [a + b for a, b in zip(t[::2], t[1::2])]
            tiles[i] = jnp.where(keep, tiles[i], 0.0) - t[0]
        padded = jnp.concatenate([rows[i - m] if m <= i < m + h else blank for i in range(n)], 0)
        change = dot(jnp.concatenate([tiles[i] for i in far], 0), padded)
        for j, i in enumerate(far):
            tiles[i] = jnp.where(keep, tiles[i], 0.0) - change[8 * j : 8 * j + 8]
        tiles[m : m + h] = rows
        share = -(-len(chores) // (n // h - 1))
        for chore in chores[m // h * share : (m // h + 1) * share]:
            chore()
    return tiles


def solve_kernel(size, pieces, damp_ref, *refs):
    nb = size // B
    got, x_ref, (pack_ref, v_ref, *panels) = refs[: 2 * pieces], refs[2 * pieces], refs[2 * pieces + 1 :]
    w_refs, z_refs = panels[:nb], panels[nb:]
    piece = got[0].shape[0]
    spots = [piece_rows(t, own, piece * pieces, piece) for own in (True, False) for t in range(pieces)]
    for ref, rows in zip(got, spots):
        pack_ref[rows, :] = ref[...]
    starts = panel_starts(size)
    factor = damp_ref[0]
    zero = jnp.minimum(jnp.full((8, B), jnp.abs(factor)), 0.0)
    lane = lax.broadcasted_iota(jnp.int32, (8, B), 1)
    sub = lax.broadcasted_iota(jnp.int32, (8, B), 0)
    for k, w_ref in enumerate(w_refs):
        rows = size - k * B
        w_ref[0:rows, :] = pack_ref[starts[k] : starts[k + 1], :]
        for side in (0, 1):
            at = starts[-2] + 2 * k + side
            w_ref[rows : rows + 8, side * (B // 2) : (side + 1) * (B // 2)] = jnp.broadcast_to(
                pack_ref[at : at + 1, B // 2 :], (8, B // 2)
            )
        if k == nb - 1:
            w_ref[0 : 2 * nb, B // 2 : B] = w_ref[B // 2 : B, :].T[0 : 2 * nb, :]
        for t in range(B // 8):
            a = w_ref[8 * t : 8 * t + 8, :]
            w_ref[8 * t : 8 * t + 8, :] = a + jnp.where(lane == sub + 8 * t, a * factor, 0.0)

    def scale(k, lo, hi):
        z_refs[k][lo:hi, :] = dot(w_refs[k][B + lo : B + hi, :], v_ref[k * B : (k + 1) * B, :])

    def update(k, j, lo, hi):
        at = (j - k) * B
        z = z_refs[k][at - B + lo : at - B + hi, :]
        w_refs[j][lo:hi, :] -= dot(z, w_refs[k][at : at + B, :], ((1,), (1,)))

    chores = []
    for k in range(nb):
        inv = inverse([w_refs[k][8 * t : 8 * t + 8, :] for t in range(B // 8)], zero, chores)
        for t in range(B // 8):
            v_ref[k * B + 8 * t : k * B + 8 * t + 8, :] = inv[t]
        below = size - (k + 1) * B
        if below:
            scale(k, 0, B)
            update(k, k + 1, 0, B)
        cuts = list(range(B if below else 0, below, B)) + [below]
        chores = [functools.partial(scale, k, lo, min(lo + B, below) if lo < below else below + 8) for lo in cuts]
        for j in range(k + 1, nb):
            rows = size - j * B
            for lo in range(B if j == k + 1 else 0, rows + 8, B):
                chores.append(functools.partial(update, k, j, lo, min(lo + B, rows) if lo < rows else rows + 8))
    for chore in chores:
        chore()
    x = [None] * nb
    for k in reversed(range(nb)):
        below = (nb - 1 - k) * B
        s = z_refs[k][below : below + 8, :]
        for j in range(k + 1, nb):
            s = s - dot(x[j], z_refs[k][(j - k - 1) * B : (j - k) * B, :])
        x[k] = s
        x_ref[0:1, k * B : (k + 1) * B] = -s[0:1]


def solve_call(size, total, damping, got):
    nb = size // B
    scratch = lambda rows: pltpu.VMEM((rows, B), jnp.float32)
    return pl.pallas_call(
        functools.partial(solve_kernel, size, len(got) // 2),
        out_shape=f32(1, size),
        in_specs=[SMEM] + [VMEM] * len(got),
        out_specs=VMEM,
        scratch_shapes=[scratch(total), scratch(size)]
        + [scratch(size - k * B + 8) for k in range(nb)]
        + [scratch(size - (k + 1) * B + 8) for k in range(nb)],
        compiler_params=pltpu.CompilerParams(vmem_limit_bytes=KERNEL_VMEM),
        name="solve",
    )(damping, *got)


def tree_sum(parts):
    while len(parts) > 1:
        parts = [a + b for a, b in zip(parts[::2], parts[1::2])]
    return parts[0]


def exchange_order(spaces):
    far = list(range(spaces - 1, spaces // 2 - 1, -1))
    return far[1::2] + list(range(2, spaces // 2)) + far[::2] + [1]


def per_device(jacobian, residual, damping):
    sensors, spaces = lax.axis_size("sensor"), lax.axis_size("space")
    part, seen = jacobian.shape
    size = part * spaces
    span = seen // spaces
    me = lax.axis_index("space")
    both = ("sensor", "space")

    def swap(x, bits):
        return lax.ppermute(x, both, [(i, i ^ bits) for i in range(sensors * spaces)])

    def panel(step):
        return lax.dynamic_slice_in_dim(jacobian, (me ^ step) * span, span, 1)

    order = exchange_order(spaces)
    first = panel(order[0])
    jacobian, first = lax.optimization_barrier((jacobian, first))
    late = dict((step, panel(step)) for step in [0] + order[1:])
    late[order[0]] = first
    got = []
    for step in order:
        got.append(swap(late[step], step))
    got = dict(zip(order, got))
    got[0] = late[0]
    seen_residual = lax.dynamic_slice_in_dim(residual, me * span, span, 0).reshape(1, span)
    cut = size // 2
    near = pl.pallas_call(
        functools.partial(near_kernel, spaces),
        out_shape=[f32(cut, span), f32(cut, cut), f32(8, cut)],
        in_specs=[VMEM] * (spaces // 2 + 1),
        out_specs=[VMEM] * 3,
        compiler_params=pltpu.CompilerParams(vmem_limit_bytes=KERNEL_VMEM),
        name="near",
    )(seen_residual, *[got[step] for step in range(spaces // 2)])

    blocks = panel_starts(size)[-1]
    unit = 16 * sensors
    total = -(-blocks // unit) * unit
    pieces = sensors
    piece = total // 2 // pieces
    packed = pl.pallas_call(
        functools.partial(gram_kernel, list(range(spaces // 2, spaces)), total, pieces),
        out_shape=[f32(piece, B)] * (2 * pieces),
        in_specs=[VMEM] * (spaces // 2 + 4),
        out_specs=[VMEM] * (2 * pieces),
        scratch_shapes=[pltpu.VMEM((cut, span), jnp.float32), pltpu.VMEM((total, B), jnp.float32)],
        compiler_params=pltpu.CompilerParams(vmem_limit_bytes=KERNEL_VMEM),
        name="gram",
    )(seen_residual, *near, *[got[step] for step in range(spaces // 2, spaces)])
    plane = [(t >> 1) * 2 * spaces + (t & 1) for t in range(pieces)]
    sums = [kept + swap(sent, spaces) for sent, kept in zip(packed[:pieces], packed[pieces:])]
    mine = tree_sum([sums[0]] + [swap(sums[t], plane[t]) for t in range(1, pieces)])
    mine = tree_sum([mine] + [swap(mine, 2 * u) for u in range(1, spaces // 2)])
    half = [mine] + [swap(mine, plane[t]) for t in range(1, pieces)]
    x = solve_call(size, total, damping, half + [swap(x, spaces) for x in half])
    return x.reshape(size)


def solution(mesh):
    placed = (P("space", "sensor"), P("sensor"), P())
    return jax.shard_map(per_device, mesh=mesh, in_specs=placed, out_specs=P(), check_vma=False)
```
